32 devices in a mesh: groups: 2 (over x), ctx: 16 (over z, y, core).
Axes of the slice: x: 2, y: 2, z: 4, core: 2. Of those that a mesh axis runs over, the one named last changes fastest.
Arguments:
- projected: bfloat16 [3, 16384, 4096], P(None, ('groups', 'ctx')), parts along dimension 1, may hold values from -6 to 6
- conv_weight: float32 [3, 4, 4096], replicated, may hold values from -3 to 3
- level_codes: int32 [14, 32, 16384], P(None, None, ('groups', 'ctx')), parts along dimension 2, may hold values from 1 to 16
- out_gain: float32 [4096], replicated, may hold values from 0.25 to 1.75
Outputs:
- mixed: bfloat16 [16384, 4096], P(('groups', 'ctx')), parts along dimension 0
The draws below stay inside these ranges and needn't reach their ends.
There are 2 independent parts, one for each index of `groups`. The reference program is written for one: setup_inputs(seed, part) draws one part's arguments, and reference() takes and returns one part's arrays. A program takes and returns all parts, laid end to end along the dimension named above; an argument that names none is the same for every part. Nothing has to cross between parts.
Inputs may be any that keep to these rules, and one draw needn't show every extreme that they name: `level_codes`: numerators of the level coefficients, which are the values divided by 8.
All inputs are finite; a program needn't handle non-finite values.
Results may differ from the reference program's by a relative error of at most 0.007.
Values may be sent and summed in bfloat16 or wider, within the bound.
A program may use at most 192 MiB of HBM per device.

```python
import jax
import jax.numpy as jnp
from jax import lax

H = 32
DH = 128
D = 4096
KW = 4
TOK_DEV = 512
TOK_BITS = 9
CTX_BITS = 4
LEVELS = 14
TOKENS = 8192
N_CTX = 16


def touch_ends(array, key, smallest, high):
    dims = array.shape
    index_at = [jax.random.randint(jax.random.fold_in(key, axis), (), 0, dims[axis]) for axis in range(len(dims))]
    array = array.at[tuple(index_at)].set(smallest)
    longest = dims.index(max(dims))
    index_at[longest] = (index_at[longest] + 1) % dims[longest]
    return array.at[tuple(index_at)].set(high)


def levels(key, shape, pieces, least, high):
    factor_of, own = 1.0, jax.random.fold_in(key, 6)
    for dim, shards_of in pieces:
        draws = jnp.exp(jax.random.uniform(jax.random.fold_in(own, dim), (shards_of,), jnp.float32, least / len(pieces), high / len(pieces)))
        factor_of = factor_of * jnp.repeat(draws, shape[dim] // shards_of).reshape([-1 if axis == dim else 1 for axis in range(len(shape))])
    return factor_of


def noise(stream_key, dims, spread, limit, split=(), dtype=jnp.bfloat16):
    result = jax.random.normal(stream_key, dims, jnp.float32) * spread
    if len(split) > 0:
        result = levels(stream_key, dims, split, -0.22, 0.18) * result
    return jnp.clip(result, min=-limit, max=limit).astype(dtype)


def setup_inputs(seed: int = 0, part: int = 0) -> dict:
    splits = jax.random.split(jax.random.key(seed), 5)
    own_keys = jax.random.split(jax.random.fold_in(splits[4], part), 5)
    return {
        "projected": noise(own_keys[0], (3, TOKENS, D), 1.0, 6.0, ((1, 16),)),
        "conv_weight": noise(splits[1], (3, KW, D), 0.5, 3.0, (), jnp.float32),
        "level_codes": touch_ends(jax.random.randint(own_keys[2], (LEVELS, H, TOKENS), 1, 17), jax.random.fold_in(own_keys[2], 1), 1, 16).astype(jnp.int32),
        "out_gain": jnp.clip(1.0 + 0.15 * jax.random.normal(splits[3], (D,), jnp.float32), 0.25, 1.75),
    }


def convolve(projected, conv_weight):
    tap_count = conv_weight.shape[1]
    row_count = projected.shape[1]
    source = projected.astype(jnp.float32)
    padded = jnp.concatenate([jnp.zeros((3, tap_count - 1, source.shape[2]), jnp.float32), source], 1)
    running = jnp.zeros(source.shape, jnp.float32)
    for offset in range(tap_count):
        running = running + conv_weight[:, offset, None, :] * padded[:, offset:offset + row_count, :]
    return running.astype(jnp.bfloat16)

def intra_levels(length, bit_count):
    position = lax.iota(jnp.int32, length)
    differ = jnp.bitwise_xor(position[:, None], position[None, :])
    level = jnp.zeros((length, length), jnp.int32)
    for exponent in range(bit_count):
        level = level + (differ >= 2 ** exponent).astype(jnp.int32)
    causal = position[None, :] <= position[:, None]
    return jnp.stack([(causal & (level == number)).astype(jnp.float32) for number in range(bit_count + 1)])

def local_layer(query_rows, key_rows, value_rows, level_weight, fenwick, onehot, out_gain):
    highest = lax.Precision.HIGHEST
    scores = jnp.einsum('thd,shd->hts', query_rows, key_rows, precision=highest)
    weight = jnp.einsum('lts,lht->hts', onehot, level_weight[:TOK_BITS + 1], precision=highest)
    weights = lax.optimization_barrier((scores * weight).astype(jnp.bfloat16)).astype(jnp.float32)
    inside = jnp.einsum('hts,shd->thd', weights, value_rows, precision=highest)
    fenwick_bf = lax.optimization_barrier(fenwick.astype(jnp.bfloat16)).astype(jnp.float32)
    across = jnp.zeros(inside.shape, jnp.float32)
    for bit_index in range(CTX_BITS):
        product = jnp.einsum('thd,hde->the', query_rows, fenwick_bf[bit_index], precision=highest)
        across = across + level_weight[TOK_BITS + 1 + bit_index].T[:, :, None] * product
    combined = inside + across
    inverse = lax.rsqrt(lax.optimization_barrier(jnp.mean(combined * combined, -1, keepdims=True)) + 1e-06)
    normed = combined * inverse * out_gain.reshape(H, DH)
    return normed.astype(jnp.bfloat16).reshape(TOK_DEV, H * DH)

def reference(projected, conv_weight, level_codes, out_gain):
    mixed_in = convolve(projected, conv_weight)
    level_weight = level_codes.astype(jnp.float32) / 8.0
    onehot = intra_levels(TOK_DEV, TOK_BITS)
    heads_all = mixed_in.reshape(3, N_CTX, TOK_DEV, H, DH).astype(jnp.float32)
    states = jnp.einsum('cshd,cshe->chde', heads_all[1], heads_all[2], precision=lax.Precision.HIGHEST)
    span_ids = lax.iota(jnp.int32, N_CTX)
    differ = jnp.bitwise_xor(span_ids[:, None], span_ids[None, :])
    earlier = span_ids[None, :] < span_ids[:, None]
    bucket_masks = jnp.stack([(earlier & (differ >= 2 ** bit_index) & (differ < 2 ** (bit_index + 1))).astype(jnp.float32) for bit_index in range(CTX_BITS)])
    outputs = []
    for span_index in range(N_CTX):
        fenwick = jnp.einsum('bs,shde->bhde', bucket_masks[:, span_index, :], states, precision=lax.Precision.HIGHEST)
        level_part = level_weight[:, :, span_index * TOK_DEV:(span_index + 1) * TOK_DEV]
        outputs.append(local_layer(heads_all[0, span_index], heads_all[1, span_index], heads_all[2, span_index], level_part, fenwick, onehot, out_gain))
    return jnp.concatenate(outputs, 0)
```

```python
import functools

import jax
import jax.numpy as jnp
from jax import lax
from jax.experimental import pallas as pl
from jax.experimental.pallas import tpu as pltpu
from jax.sharding import PartitionSpec as P

PAD = 8
TILE = 128
NT = (((1,), (1,)), ((), ()))


def convolve(data_ref, rim_ref, taps_ref, held):
    rows = data_ref.shape[1]
    taps = taps_ref.shape[1]
    held[0:PAD, :] = rim_ref[0]
    held[PAD : PAD + rows, :] = data_ref[0].astype(jnp.float32)
    total = taps_ref[0, 0:1, :] * held[PAD - taps + 1 : PAD - taps + 1 + rows, :]
    for tap in range(1, taps):
        first = PAD - taps + 1 + tap
        total = total + taps_ref[0, tap : tap + 1, :] * held[first : first + rows, :]
    return total.astype(jnp.bfloat16)


def state_kernel(dim, k_in, v_in, k_rim, v_rim, k_taps, v_taps, k_out, vt_out, state_out, held):
    k_out[...] = convolve(k_in, k_rim, k_taps, held)
    values = convolve(v_in, v_rim, v_taps, held)
    for head in range(k_out.shape[1] // dim):
        lanes = slice(head * dim, (head + 1) * dim)
        flipped = values[:, lanes].T
        vt_out[lanes, :] = flipped
        state_out[head] = jnp.dot(
            flipped, k_out[:, lanes], preferred_element_type=jnp.float32
        ).astype(jnp.bfloat16)


def tile_weights(lam, rows):
    strip = PAD.bit_length() - 1
    query = lax.rem(lax.broadcasted_iota(jnp.int32, (TILE // PAD, rows), 1), TILE)
    block = lax.broadcasted_iota(jnp.int32, (TILE // PAD, rows), 0)
    differ = lax.bitwise_xor(lax.shift_right_logical(query, strip), block)
    top = TILE.bit_length() - 1
    outer = jnp.broadcast_to(lam[top : top + 1], differ.shape)
    for level in range(top - 1, strip, -1):
        outer = jnp.where(differ < 2 ** (level - strip), lam[level : level + 1], outer)
    outer = jnp.where(block <= lax.shift_right_logical(query, strip), outer, 0.0)
    query8 = lax.rem(lax.broadcasted_iota(jnp.int32, (PAD, rows), 1), PAD)
    key8 = lax.broadcasted_iota(jnp.int32, (PAD, rows), 0)
    differ8 = lax.bitwise_xor(query8, key8)
    inner = jnp.broadcast_to(lam[strip : strip + 1], differ8.shape)
    for level in range(strip - 1, -1, -1):
        inner = jnp.where(differ8 < 2**level, lam[level : level + 1], inner)
    inner = jnp.where(key8 <= query8, inner, 0.0)
    own = lax.shift_right_logical(
        lax.rem(lax.broadcasted_iota(jnp.int32, (PAD, rows), 1), TILE), strip
    )
    return jnp.concatenate(
        [
            jnp.where(own == number, inner, outer[number : number + 1])
            for number in range(TILE // PAD)
        ],
        0,
    )


def inside_kernel(dim, q_in, q_rim, q_taps, k_in, vt_in, lam_in, q_old, in_old, q_out, in_out, held, weights):
    rows = k_in.shape[0]
    tiles = rows // TILE
    q_out[...] = convolve(q_in, q_rim, q_taps, held)
    top = TILE.bit_length() - 1
    pair = min(2, tiles)
    for tile in range(tiles):
        start = tile // pair * pair * TILE
        if start < tile * TILE:
            weights[tile * TILE : (tile + 1) * TILE, start : tile * TILE] = jnp.zeros(
                (TILE, tile * TILE - start), jnp.bfloat16
            )
    for head in range(k_in.shape[1] // dim):
        lanes = slice(head * dim, (head + 1) * dim)
        lam = lam_in[head]
        diagonal = tile_weights(lam, rows)
        for tile in range(tiles):
            keys = slice(tile * TILE, (tile + 1) * TILE)
            scores = lax.dot_general(
                k_in[keys, lanes],
                q_out[tile * TILE :, lanes],
                NT,
                preferred_element_type=jnp.float32,
            )
            for other in range(tile, tiles):
                queries = slice(other * TILE, (other + 1) * TILE)
                part = scores[:, (other - tile) * TILE : (other - tile + 1) * TILE]
                if other == tile:
                    factor = diagonal[:, queries]
                else:
                    level = top + (other ^ tile).bit_length()
                    factor = lam[level : level + 1, queries]
                weights[keys, queries] = (part * factor).astype(jnp.bfloat16)
        for first in range(0, tiles, pair):
            queries = slice(first * TILE, (first + pair) * TILE)
            depth = (first + pair) * TILE
            in_out[lanes, queries] = jnp.dot(
                vt_in[lanes, :depth], weights[:depth, queries], preferred_element_type=jnp.float32
            )


def mix_kernel(dim, base, bits, q_in, in_in, lam_in, gain_in, *rest):
    levels, out = rest[:bits], rest[bits]
    for head in range(q_in.shape[1] // dim):
        lanes = slice(head * dim, (head + 1) * dim)
        total = in_in[lanes, :]
        for bit in range(bits):
            product = lax.dot_general(
                levels[bit][head], q_in[:, lanes], NT, preferred_element_type=jnp.float32
            )
            total = total + lam_in[head, base + bit : base + bit + 1, :] * product
        inverse = lax.rsqrt(jnp.mean(total * total, 0, keepdims=True) + 1e-06)
        normed = (total * inverse).T * gain_in[0:1, lanes]
        out[:, lanes] = normed.astype(jnp.bfloat16)


def fenwick_levels(state):
    count = lax.axis_size("ctx")
    bits = count.bit_length() - 1
    me = lax.axis_index("ctx")
    heads = state.shape[0]
    found = []
    for bit in range(bits):
        depth = (bit + 1) // 2
        last = bit == bits - 1
        size = heads // 2**depth
        piece = state
        if depth:
            piece = lax.dynamic_slice_in_dim(state, (me & (2**depth - 1)) * size, size, 0)
        takers = [to for to in range(count) if not last or to >> bit & 1]
        got = lax.ppermute(piece, "ctx", [(to ^ 2**bit, to) for to in takers])
        for step in range(depth):
            other = lax.ppermute(got, "ctx", [(to ^ 2**step, to) for to in takers])
            got = jnp.where(
                (me >> step) & 1 == 1,
                jnp.concatenate([other, got], 0),
                jnp.concatenate([got, other], 0),
            )
        found.append(got)
        if not last:
            state = (state.astype(jnp.float32) + got.astype(jnp.float32)).astype(jnp.bfloat16)
    return found


def on_device(projected, conv_weight, level_codes, out_gain):
    taps = conv_weight.shape[1]
    rows, width = projected.shape[1:]
    level_count, heads = level_codes.shape[:2]
    dim = width // heads
    tok_bits = rows.bit_length() - 1
    count = lax.axis_size("ctx")
    bits = count.bit_length() - 1
    me = lax.axis_index("ctx")
    group = 4 if heads % 4 == 0 else 1
    lanes = group * dim
    steps = heads // group

    rim = lax.ppermute(
        projected[:, rows - taps + 1 :, :], "ctx", [(c, c + 1) for c in range(count - 1)]
    )
    rim = jnp.pad(rim.astype(jnp.float32), ((0, 0), (PAD - taps + 1, 0), (0, 0)))
    on_bit = (me >> jnp.arange(bits)) & 1
    scale = jnp.concatenate([jnp.ones((tok_bits + 1,), jnp.int32), on_bit])
    lam = (level_codes * scale[:, None, None]).transpose(1, 0, 2).astype(jnp.float32) / 8.0

    def data(kind, base=0):
        return [
            pl.BlockSpec((1, rows, lanes), lambda g: (kind, 0, g + base)),
            pl.BlockSpec((1, PAD, lanes), lambda g: (kind, 0, g + base)),
            pl.BlockSpec((1, taps, lanes), lambda g: (kind, 0, g + base)),
        ]

    def wide(base=0):
        return pl.BlockSpec((rows, lanes), lambda g: (0, g + base))

    def tall(base=0):
        return pl.BlockSpec((lanes, rows), lambda g: (g + base, 0))

    def per_head(size, base=0):
        return pl.BlockSpec((group,) + size, lambda g: (g + base, 0, 0))

    k_specs, v_specs = data(1), data(2)
    held = pltpu.VMEM((PAD + rows, lanes), jnp.float32)
    limit = pltpu.CompilerParams(vmem_limit_bytes=48 * 2**20)
    keys, values_t, state = pl.pallas_call(
        functools.partial(state_kernel, dim),
        grid=(steps,),
        in_specs=[s for both in zip(k_specs, v_specs) for s in both],
        out_specs=[wide(), tall(), per_head((dim, dim))],
        out_shape=[
            jax.ShapeDtypeStruct((rows, width), jnp.bfloat16),
            jax.ShapeDtypeStruct((width, rows), jnp.bfloat16),
            jax.ShapeDtypeStruct((heads, dim, dim), jnp.bfloat16),
        ],
        scratch_shapes=[held],
        compiler_params=limit,
        name="states",
    )(projected, projected, rim, rim, conv_weight, conv_weight)

    levels = fenwick_levels(state)

    parts = 4 if steps % 4 == 0 else 1
    own = steps // parts
    shapes = [
        jax.ShapeDtypeStruct((rows, width), jnp.bfloat16),
        jax.ShapeDtypeStruct((width, rows), jnp.float32),
    ]
    done = []
    for part in range(parts):
        base = part * own
        share = rows * rows * width // parts
        call = pl.pallas_call(
            functools.partial(inside_kernel, dim)
            if done
            else lambda *refs: inside_kernel(dim, *refs[:6], None, None, *refs[6:]),
            grid=(own,),
            in_specs=data(0, base)
            + [wide(base), tall(base), per_head((level_count, rows), base)]
            + [pl.BlockSpec(memory_space=pl.ANY)] * len(done),
            out_specs=[wide(base), tall(base)],
            out_shape=shapes,
            scratch_shapes=[held, pltpu.VMEM((rows, rows), jnp.bfloat16)],
            input_output_aliases={6: 0, 7: 1} if done else {},
            compiler_params=limit,
            cost_estimate=pl.CostEstimate(
                flops=8 * share, bytes_accessed=10 * rows * width // parts, transcendentals=0
            ),
            name="inside",
        )
        done = list(call(projected, rim, conv_weight, keys, values_t, lam, *done))
    queries, inside = done

    return pl.pallas_call(
        functools.partial(mix_kernel, dim, tok_bits + 1, bits),
        grid=(steps,),
        in_specs=[
            wide(),
            tall(),
            per_head((level_count, rows)),
            pl.BlockSpec((1, lanes), lambda g: (0, g)),
        ]
        + [per_head((dim, dim))] * bits,
        out_specs=wide(),
        out_shape=jax.ShapeDtypeStruct((rows, width), jnp.bfloat16),
        compiler_params=limit,
        name="mix",
    )(queries, inside, lam, out_gain.reshape(1, width), *levels)


def solution(mesh):
    placed = (P(None, ("groups", "ctx"), None), P(), P(None, None, ("groups", "ctx")), P())
    return jax.shard_map(
        on_device, mesh=mesh, in_specs=placed, out_specs=P(("groups", "ctx"), None), check_vma=False
    )
```

```python
import functools

import jax
import jax.numpy as jnp
from jax import lax
from jax.experimental import pallas as pl
from jax.experimental.pallas import tpu as pltpu
from jax.sharding import PartitionSpec as P

PAD = 8
TILE = 128
NT = (((1,), (1,)), ((), ()))


def convolve(data_ref, rim_ref, taps_ref, held):
    rows = data_ref.shape[1]
    taps = taps_ref.shape[1]
    held[0:PAD, :] = rim_ref[0]
    held[PAD : PAD + rows, :] = data_ref[0].astype(jnp.float32)
    total = taps_ref[0, 0:1, :] * held[PAD - taps + 1 : PAD - taps + 1 + rows, :]
    for tap in range(1, taps):
        first = PAD - taps + 1 + tap
        total = total + taps_ref[0, tap : tap + 1, :] * held[first : first + rows, :]
    return total.astype(jnp.bfloat16)


def state_kernel(dim, k_in, v_in, k_rim, v_rim, k_taps, v_taps, k_out, vt_out, state_out, held):
    k_out[...] = convolve(k_in, k_rim, k_taps, held)
    values = convolve(v_in, v_rim, v_taps, held)
    for head in range(k_out.shape[1] // dim):
        lanes = slice(head * dim, (head + 1) * dim)
        flipped = values[:, lanes].T
        vt_out[lanes, :] = flipped
        state_out[head] = jnp.dot(
            flipped, k_out[:, lanes], preferred_element_type=jnp.float32
        ).astype(jnp.bfloat16)


def tile_weights(lam, rows):
    strip = PAD.bit_length() - 1
    query = lax.rem(lax.broadcasted_iota(jnp.int32, (TILE // PAD, rows), 1), TILE)
    block = lax.broadcasted_iota(jnp.int32, (TILE // PAD, rows), 0)
    differ = lax.bitwise_xor(lax.shift_right_logical(query, strip), block)
    top = TILE.bit_length() - 1
    outer = jnp.broadcast_to(lam[top : top + 1], differ.shape)
    for level in range(top - 1, strip, -1):
        outer = jnp.where(differ < 2 ** (level - strip), lam[level : level + 1], outer)
    outer = jnp.where(block <= lax.shift_right_logical(query, strip), outer, 0.0)
    query8 = lax.rem(lax.broadcasted_iota(jnp.int32, (PAD, rows), 1), PAD)
    key8 = lax.broadcasted_iota(jnp.int32, (PAD, rows), 0)
    differ8 = lax.bitwise_xor(query8, key8)
    inner = jnp.broadcast_to(lam[strip : strip + 1], differ8.shape)
    for level in range(strip - 1, -1, -1):
        inner = jnp.where(differ8 < 2**level, lam[level : level + 1], inner)
    inner = jnp.where(key8 <= query8, inner, 0.0)
    own = lax.shift_right_logical(
        lax.rem(lax.broadcasted_iota(jnp.int32, (PAD, rows), 1), TILE), strip
    )
    return jnp.concatenate(
        [
            jnp.where(own == number, inner, outer[number : number + 1])
            for number in range(TILE // PAD)
        ],
        0,
    )


def inside_kernel(dim, q_in, q_rim, q_taps, k_in, vt_in, lam_in, q_old, in_old, q_out, in_out, held, weights):
    rows = k_in.shape[0]
    tiles = rows // TILE
    q_out[...] = convolve(q_in, q_rim, q_taps, held)
    top = TILE.bit_length() - 1
    pair = min(2, tiles)
    for tile in range(tiles):
        start = tile // pair * pair * TILE
        if start < tile * TILE:
            weights[tile * TILE : (tile + 1) * TILE, start : tile * TILE] = jnp.zeros(
                (TILE, tile * TILE - start), jnp.bfloat16
            )
    for head in range(k_in.shape[1] // dim):
        lanes = slice(head * dim, (head + 1) * dim)
        lam = lam_in[head]
        diagonal = tile_weights(lam, rows)
        for tile in range(tiles):
            keys = slice(tile * TILE, (tile + 1) * TILE)
            scores = lax.dot_general(
                k_in[keys, lanes],
                q_out[tile * TILE :, lanes],
                NT,
                preferred_element_type=jnp.float32,
            )
            for other in range(tile, tiles):
                queries = slice(other * TILE, (other + 1) * TILE)
                part = scores[:, (other - tile) * TILE : (other - tile + 1) * TILE]
                if other == tile:
                    factor = diagonal[:, queries]
                else:
                    level = top + (other ^ tile).bit_length()
                    factor = lam[level : level + 1, queries]
                weights[keys, queries] = (part * factor).astype(jnp.bfloat16)
        for first in range(0, tiles, pair):
            queries = slice(first * TILE, (first + pair) * TILE)
            depth = (first + pair) * TILE
            in_out[lanes, queries] = jnp.dot(
                vt_in[lanes, :depth], weights[:depth, queries], preferred_element_type=jnp.float32
            )


def mix_kernel(dim, base, bits, q_in, in_in, lam_in, gain_in, *rest):
    levels, out = rest[:bits], rest[bits]
    for head in range(q_in.shape[1] // dim):
        lanes = slice(head * dim, (head + 1) * dim)
        total = in_in[lanes, :]
        for bit in range(bits):
            product = lax.dot_general(
                levels[bit][head], q_in[:, lanes], NT, preferred_element_type=jnp.float32
            )
            total = total + lam_in[head, base + bit : base + bit + 1, :] * product
        inverse = lax.rsqrt(jnp.mean(total * total, 0, keepdims=True) + 1e-06)
        normed = (total * inverse).T * gain_in[0:1, lanes]
        out[:, lanes] = normed.astype(jnp.bfloat16)


class Chain:
    def __init__(self):
        self.count = lax.axis_size("ctx")
        self.bits = self.count.bit_length() - 1
        self.me = lax.axis_index("ctx")
        self.state, self.got, self.found = None, None, []

    def piece(self, bit):
        depth = (bit + 1) // 2
        if not depth:
            return self.state
        size = self.state.shape[0] // 2**depth
        index = 0
        for step in range(depth):
            index = index + (((self.me >> step) & 1) << (depth - 1 - step))
        return lax.dynamic_slice_in_dim(self.state, index * size, size, 0)

    def operations(self, bit):
        return [(bit, None)] + [(bit, step) for step in reversed(range((bit + 1) // 2))]

    def takers(self, bit):
        return [to for to in range(self.count) if bit < self.bits - 1 or to >> bit & 1]

    def outgoing(self, operation):
        bit, step = operation
        return self.piece(bit) if step is None else self.got

    def exchange(self, operation, value):
        bit, step = operation
        away = 2**bit if step is None else 2**step
        return lax.ppermute(value, "ctx", [(to ^ away, to) for to in self.takers(bit)])

    def land(self, operation, value, came):
        bit, step = operation
        if step is None:
            self.got = came
        else:
            self.got = jnp.where(
                (self.me >> step) & 1 == 1,
                jnp.concatenate([came, value], 0),
                jnp.concatenate([value, came], 0),
            )
        if operation == self.operations(bit)[-1]:
            self.found.append(self.got)
            if bit < self.bits - 1:
                total = self.state.astype(jnp.float32) + self.got.astype(jnp.float32)
                self.state = total.astype(jnp.bfloat16)


def tie(values):
    return lax.optimization_barrier(values)


def stage(moves, compute, inputs):
    values, inputs = tie(([chain.outgoing(op) for chain, op in moves], inputs))
    came = [chain.exchange(op, value) for (chain, op), value in zip(moves, values)]
    results = compute(inputs) if compute else inputs
    came, values, results = tie((came, values, results))
    for (chain, op), value, new in zip(moves, values, came):
        chain.land(op, value, new)
    return results


def on_device(projected, conv_weight, level_codes, out_gain):
    taps = conv_weight.shape[1]
    rows, width = projected.shape[1:]
    level_count, heads = level_codes.shape[:2]
    dim = width // heads
    tok_bits = rows.bit_length() - 1
    count = lax.axis_size("ctx")
    bits = count.bit_length() - 1
    me = lax.axis_index("ctx")
    group = 4
    lanes = group * dim
    halves, parts = 2, 4
    steps = heads // group // halves

    rim = lax.ppermute(
        projected[:, rows - taps + 1 :, :], "ctx", [(c, c + 1) for c in range(count - 1)]
    )
    on_bit = (me >> jnp.arange(bits)) & 1
    scale = jnp.concatenate([jnp.ones((tok_bits + 1,), jnp.int32), on_bit])
    lam = (level_codes * scale[:, None, None]).transpose(1, 0, 2).astype(jnp.float32) / 8.0
    rim, lam = tie((rim, lam))
    rim = jnp.pad(rim.astype(jnp.float32), ((0, 0), (PAD - taps + 1, 0), (0, 0)))

    def data(kind, base):
        return [
            pl.BlockSpec((1, rows, lanes), lambda g: (kind, 0, g + base)),
            pl.BlockSpec((1, PAD, lanes), lambda g: (kind, 0, g + base)),
            pl.BlockSpec((1, taps, lanes), lambda g: (kind, 0, g + base)),
        ]

    def wide(base=0):
        return pl.BlockSpec((rows, lanes), lambda g: (0, g + base))

    def tall(base=0):
        return pl.BlockSpec((lanes, rows), lambda g: (g + base, 0))

    def per_head(size, base=0):
        return pl.BlockSpec((group,) + size, lambda g: (g + base, 0, 0))

    held = pltpu.VMEM((PAD + rows, lanes), jnp.float32)
    limit = pltpu.CompilerParams(vmem_limit_bytes=56 * 2**20)
    half_width = width // halves

    def states(half, rim):
        base = half * steps
        return pl.pallas_call(
            functools.partial(state_kernel, dim),
            grid=(steps,),
            in_specs=[s for both in zip(data(1, base), data(2, base)) for s in both],
            out_specs=[wide(), tall(), per_head((dim, dim))],
            out_shape=[
                jax.ShapeDtypeStruct((rows, half_width), jnp.bfloat16),
                jax.ShapeDtypeStruct((half_width, rows), jnp.bfloat16),
                jax.ShapeDtypeStruct((heads // halves, dim, dim), jnp.bfloat16),
            ],
            scratch_shapes=[held],
            compiler_params=limit,
            cost_estimate=pl.CostEstimate(
                flops=2 * rows * half_width * dim,
                bytes_accessed=8 * rows * half_width,
                transcendentals=0,
            ),
            name="states",
        )(projected, projected, rim, rim, conv_weight, conv_weight)

    def inside(part, rim, keys, values_t, lam, done):
        own = steps * halves // parts
        within = part % (parts // halves) * own
        share = rows * rows * width // parts
        call = pl.pallas_call(
            functools.partial(inside_kernel, dim)
            if done
            else lambda *refs: inside_kernel(dim, *refs[:6], None, None, *refs[6:]),
            grid=(own,),
            in_specs=data(0, part * own)
            + [wide(within), tall(within), per_head((level_count, rows), part * own)]
            + [pl.BlockSpec(memory_space=pl.ANY)] * len(done),
            out_specs=[wide(within), tall(within)],
            out_shape=[
                jax.ShapeDtypeStruct((rows, half_width), jnp.bfloat16),
                jax.ShapeDtypeStruct((half_width, rows), jnp.float32),
            ],
            scratch_shapes=[held, pltpu.VMEM((rows, rows), jnp.bfloat16)],
            input_output_aliases={6: 0, 7: 1} if done else {},
            compiler_params=limit,
            cost_estimate=pl.CostEstimate(
                flops=8 * share, bytes_accessed=10 * rows * width // parts, transcendentals=0
            ),
            name="inside",
        )
        return list(call(projected, rim, conv_weight, keys, values_t, lam, *done))

    def mix(half, queries, within, lam, levels, done):
        base = half * steps
        kernel = functools.partial(mix_kernel, dim, tok_bits + 1, bits)
        if done:
            kernel = lambda *refs: mix_kernel(
                dim, tok_bits + 1, bits, *refs[: 4 + bits], refs[-1]
            )
        return pl.pallas_call(
            kernel,
            grid=(steps,),
            in_specs=[
                wide(),
                tall(),
                per_head((level_count, rows), base),
                pl.BlockSpec((1, lanes), lambda g: (0, g + base)),
            ]
            + [per_head((dim, dim))] * bits
            + [pl.BlockSpec(memory_space=pl.ANY)] * len(done),
            out_specs=wide(base),
            out_shape=jax.ShapeDtypeStruct((rows, width), jnp.bfloat16),
            input_output_aliases={4 + bits: 0} if done else {},
            compiler_params=limit,
            cost_estimate=pl.CostEstimate(
                flops=2 * bits * rows * half_width * dim,
                bytes_accessed=8 * rows * half_width,
                transcendentals=0,
            ),
            name="mix",
        )(queries, within, lam, out_gain.reshape(1, width), *levels, *done)

    first, second = Chain(), Chain()
    keys, values_t = [None] * halves, [None] * halves
    keys[0], values_t[0], first.state = states(0, rim)
    keys[1], values_t[1], second.state = stage(
        [(first, op) for op in first.operations(0)], lambda r: states(1, r), rim
    )
    done = [[], []]
    waiting = list(range(parts))
    for turn in range(1, bits + 1):
        early = first.operations(turn) if turn < bits else []
        late = second.operations(turn - 1)
        todo = [waiting.pop(0)] if waiting else []
        if turn == bits:
            todo, waiting = todo + waiting, []
        for index in range(max(len(early), len(late))):
            moves = [(first, op) for op in early[index : index + 1]]
            moves += [(second, op) for op in late[index : index + 1]]
            if index == 0 and todo:

                def run(inputs):
                    lam, done = inputs
                    done = list(done)
                    for part in todo:
                        half = part * halves // parts
                        done[half] = inside(part, rim, keys[half], values_t[half], lam, done[half])
                    return lam, done

                lam, done = stage(moves, run, (lam, done))
            elif turn == bits and index == 1:

                def run(inputs):
                    lam, (queries, within), levels = inputs
                    return mix(0, queries, within, lam, levels, [])

                out = stage(moves, run, (lam, done[0], first.found))
            else:
                lam, done = stage(moves, None, (lam, done))
    return mix(1, *done[1], lam, second.found, [out])


def solution(mesh):
    placed = (P(None, ("groups", "ctx"), None), P(), P(None, None, ("groups", "ctx")), P())
    return jax.shard_map(
        on_device, mesh=mesh, in_specs=placed, out_specs=P(("groups", "ctx"), None), check_vma=False
    )
```

```python
import functools

import jax
import jax.numpy as jnp
from jax import lax
from jax.experimental import pallas as pl
from jax.experimental.pallas import tpu as pltpu
from jax.sharding import PartitionSpec as P

PAD = 8
TILE = 128
NT = (((1,), (1,)), ((), ()))


def convolve(data_ref, rim_ref, taps_ref, held):
    rows = data_ref.shape[1]
    taps = taps_ref.shape[1]
    held[0:PAD, :] = rim_ref[0]
    held[PAD : PAD + rows, :] = data_ref[0].astype(jnp.float32)
    total = taps_ref[0, 0:1, :] * held[PAD - taps + 1 : PAD - taps + 1 + rows, :]
    for tap in range(1, taps):
        first = PAD - taps + 1 + tap
        total = total + taps_ref[0, tap : tap + 1, :] * held[first : first + rows, :]
    return total.astype(jnp.bfloat16)


def state_kernel(dim, k_in, v_in, k_rim, v_rim, k_taps, v_taps, k_out, vt_out, state_out, held):
    k_out[...] = convolve(k_in, k_rim, k_taps, held)
    values = convolve(v_in, v_rim, v_taps, held)
    for head in range(k_out.shape[1] // dim):
        lanes = slice(head * dim, (head + 1) * dim)
        flipped = values[:, lanes].T
        vt_out[lanes, :] = flipped
        state_out[head] = jnp.dot(
            flipped, k_out[:, lanes], preferred_element_type=jnp.float32
        ).astype(jnp.bfloat16)


def tile_weights(lam, rows):
    strip = PAD.bit_length() - 1
    query = lax.rem(lax.broadcasted_iota(jnp.int32, (TILE // PAD, rows), 1), TILE)
    block = lax.broadcasted_iota(jnp.int32, (TILE // PAD, rows), 0)
    differ = lax.bitwise_xor(lax.shift_right_logical(query, strip), block)
    top = TILE.bit_length() - 1
    outer = jnp.broadcast_to(lam[top : top + 1], differ.shape)
    for level in range(top - 1, strip, -1):
        outer = jnp.where(differ < 2 ** (level - strip), lam[level : level + 1], outer)
    outer = jnp.where(block <= lax.shift_right_logical(query, strip), outer, 0.0)
    query8 = lax.rem(lax.broadcasted_iota(jnp.int32, (PAD, rows), 1), PAD)
    key8 = lax.broadcasted_iota(jnp.int32, (PAD, rows), 0)
    differ8 = lax.bitwise_xor(query8, key8)
    inner = jnp.broadcast_to(lam[strip : strip + 1], differ8.shape)
    for level in range(strip - 1, -1, -1):
        inner = jnp.where(differ8 < 2**level, lam[level : level + 1], inner)
    inner = jnp.where(key8 <= query8, inner, 0.0)
    own = lax.shift_right_logical(
        lax.rem(lax.broadcasted_iota(jnp.int32, (PAD, rows), 1), TILE), strip
    )
    return jnp.concatenate(
        [
            jnp.where(own == number, inner, outer[number : number + 1])
            for number in range(TILE // PAD)
        ],
        0,
    )


def inside_kernel(dim, q_in, q_rim, q_taps, k_in, vt_in, lam_in, q_old, in_old, q_out, in_out, held, weights):
    rows = k_in.shape[0]
    tiles = rows // TILE
    q_out[...] = convolve(q_in, q_rim, q_taps, held)
    top = TILE.bit_length() - 1
    pair = min(2, tiles)
    for tile in range(tiles):
        start = tile // pair * pair * TILE
        if start < tile * TILE:
            weights[tile * TILE : (tile + 1) * TILE, start : tile * TILE] = jnp.zeros(
                (TILE, tile * TILE - start), jnp.bfloat16
            )
    for head in range(k_in.shape[1] // dim):
        lanes = slice(head * dim, (head + 1) * dim)
        lam = lam_in[head]
        diagonal = tile_weights(lam, rows)
        for tile in range(tiles):
            keys = slice(tile * TILE, (tile + 1) * TILE)
            scores = lax.dot_general(
                k_in[keys, lanes],
                q_out[tile * TILE :, lanes],
                NT,
                preferred_element_type=jnp.float32,
            )
            for other in range(tile, tiles):
                queries = slice(other * TILE, (other + 1) * TILE)
                part = scores[:, (other - tile) * TILE : (other - tile + 1) * TILE]
                if other == tile:
                    factor = diagonal[:, queries]
                else:
                    level = top + (other ^ tile).bit_length()
                    factor = lam[level : level + 1, queries]
                weights[keys, queries] = (part * factor).astype(jnp.bfloat16)
        for first in range(0, tiles, pair):
            queries = slice(first * TILE, (first + pair) * TILE)
            depth = (first + pair) * TILE
            in_out[lanes, queries] = jnp.dot(
                vt_in[lanes, :depth], weights[:depth, queries], preferred_element_type=jnp.float32
            )


def mix_kernel(dim, base, bits, q_in, in_in, lam_in, gain_in, *rest):
    levels, out = rest[:bits], rest[bits]
    for head in range(q_in.shape[1] // dim):
        lanes = slice(head * dim, (head + 1) * dim)
        total = in_in[lanes, :]
        stacked = jnp.concatenate([level[head] for level in levels], 0)
        products = lax.dot_general(
            stacked, q_in[:, lanes], NT, preferred_element_type=jnp.float32
        )
        for bit in range(bits):
            product = products[bit * dim : (bit + 1) * dim]
            total = total + lam_in[head, base + bit : base + bit + 1, :] * product
        inverse = lax.rsqrt(jnp.mean(total * total, 0, keepdims=True) + 1e-06)
        normed = (total * inverse).T * gain_in[0:1, lanes]
        out[:, lanes] = normed.astype(jnp.bfloat16)


class Chain:
    def __init__(self):
        self.count = lax.axis_size("ctx")
        self.bits = self.count.bit_length() - 1
        self.me = lax.axis_index("ctx")
        self.state, self.depth, self.got = None, 0, {}

    def operations(self, bit):
        return [(bit, None)] + [(bit, step) for step in reversed(range((bit + 1) // 2))]

    def takers(self, bit):
        return [to for to in range(self.count) if bit < self.bits - 1 or to >> bit & 1]

    def outgoing(self, operation):
        bit, step = operation
        if step is not None:
            return self.got[bit]
        while self.depth < (bit + 1) // 2:
            size = self.state.shape[0] // 2
            start = ((self.me >> self.depth) & 1) * size
            self.state = lax.dynamic_slice_in_dim(self.state, start, size, 0)
            self.depth += 1
        return self.state

    def exchange(self, operation, value):
        bit, step = operation
        away = 2**bit if step is None else 2**step
        return lax.ppermute(value, "ctx", [(to ^ away, to) for to in self.takers(bit)])

    def land(self, operation, value, came):
        bit, step = operation
        if step is None:
            self.got[bit] = came
            if bit < self.bits - 1:
                total = value.astype(jnp.float32) + came.astype(jnp.float32)
                self.state = total.astype(jnp.bfloat16)
        else:
            self.got[bit] = jnp.where(
                (self.me >> step) & 1 == 1,
                jnp.concatenate([came, value], 0),
                jnp.concatenate([value, came], 0),
            )

    def levels(self):
        return [self.got[bit] for bit in range(self.bits)]


def tie(values):
    return lax.optimization_barrier(values)


def stage(moves, compute, inputs):
    values, inputs = tie(([chain.outgoing(op) for chain, op in moves], inputs))
    came = [chain.exchange(op, value) for (chain, op), value in zip(moves, values)]
    results = compute(inputs) if compute else inputs
    came, values, results = tie((came, values, results))
    for (chain, op), value, new in zip(moves, values, came):
        chain.land(op, value, new)
    return results


def spread(groups, rounds):
    half = len(groups) // 2
    early = rounds // 2
    calls = []
    for base, count in ((0, early), (half, rounds - early)):
        for index in range(count):
            start = -(-half * index // count)
            stop = -(-half * (index + 1) // count)
            calls.append([(base + start, stop - start)] if stop > start else [])
    return calls


def on_device(projected, conv_weight, level_codes, out_gain):
    taps = conv_weight.shape[1]
    rows, width = projected.shape[1:]
    level_count, heads = level_codes.shape[:2]
    dim = width // heads
    tok_bits = rows.bit_length() - 1
    count = lax.axis_size("ctx")
    bits = count.bit_length() - 1
    me = lax.axis_index("ctx")
    group = 4
    lanes = group * dim
    halves = 2
    steps = heads // group // halves

    rim = lax.ppermute(
        projected[:, rows - taps + 1 :, :], "ctx", [(c, c + 1) for c in range(count - 1)]
    )
    on_bit = (me >> jnp.arange(bits)) & 1
    scale = jnp.concatenate([jnp.ones((tok_bits + 1,), jnp.int32), on_bit])
    lam = (level_codes * scale[:, None, None]).transpose(1, 0, 2).astype(jnp.float32) / 8.0
    rim, lam = tie((rim, lam))
    rim = jnp.pad(rim.astype(jnp.float32), ((0, 0), (PAD - taps + 1, 0), (0, 0)))

    def data(kind, base):
        return [
            pl.BlockSpec((1, rows, lanes), lambda g: (kind, 0, g + base)),
            pl.BlockSpec((1, PAD, lanes), lambda g: (kind, 0, g + base)),
            pl.BlockSpec((1, taps, lanes), lambda g: (kind, 0, g + base)),
        ]

    def wide(base=0):
        return pl.BlockSpec((rows, lanes), lambda g: (0, g + base))

    def tall(base=0):
        return pl.BlockSpec((lanes, rows), lambda g: (g + base, 0))

    def per_head(size, base=0):
        return pl.BlockSpec((group,) + size, lambda g: (g + base, 0, 0))

    held = pltpu.VMEM((PAD + rows, lanes), jnp.float32)
    limit = pltpu.CompilerParams(vmem_limit_bytes=56 * 2**20)
    half_width = width // halves

    def states(half, rim):
        base = half * steps
        return pl.pallas_call(
            functools.partial(state_kernel, dim),
            grid=(steps,),
            in_specs=[s for both in zip(data(1, base), data(2, base)) for s in both],
            out_specs=[wide(), tall(), per_head((dim, dim))],
            out_shape=[
                jax.ShapeDtypeStruct((rows, half_width), jnp.bfloat16),
                jax.ShapeDtypeStruct((half_width, rows), jnp.bfloat16),
                jax.ShapeDtypeStruct((heads // halves, dim, dim), jnp.bfloat16),
            ],
            scratch_shapes=[held],
            compiler_params=limit,
            cost_estimate=pl.CostEstimate(
                flops=2 * rows * half_width * dim,
                bytes_accessed=8 * rows * half_width,
                transcendentals=0,
            ),
            name="states",
        )(projected, projected, rim, rim, conv_weight, conv_weight)

    def inside(first_group, own, rim, keys, values_t, lam, done):
        within = first_group % steps
        share = rows * rows * lanes * own
        call = pl.pallas_call(
            functools.partial(inside_kernel, dim)
            if done
            else lambda *refs: inside_kernel(dim, *refs[:6], None, None, *refs[6:]),
            grid=(own,),
            in_specs=data(0, first_group)
            + [wide(within), tall(within), per_head((level_count, rows), first_group)]
            + [pl.BlockSpec(memory_space=pl.ANY)] * len(done),
            out_specs=[wide(within), tall(within)],
            out_shape=[
                jax.ShapeDtypeStruct((rows, half_width), jnp.bfloat16),
                jax.ShapeDtypeStruct((half_width, rows), jnp.float32),
            ],
            scratch_shapes=[held, pltpu.VMEM((rows, rows), jnp.bfloat16)],
            input_output_aliases={6: 0, 7: 1} if done else {},
            compiler_params=limit,
            cost_estimate=pl.CostEstimate(
                flops=8 * share, bytes_accessed=10 * rows * lanes * own, transcendentals=0
            ),
            name="inside",
        )
        return list(call(projected, rim, conv_weight, keys, values_t, lam, *done))

    def mix(half, queries, within, lam, levels, done):
        base = half * steps
        kernel = functools.partial(mix_kernel, dim, tok_bits + 1, bits)
        if done:
            kernel = lambda *refs: mix_kernel(
                dim, tok_bits + 1, bits, *refs[: 4 + bits], refs[-1]
            )
        return pl.pallas_call(
            kernel,
            grid=(steps,),
            in_specs=[
                wide(),
                tall(),
                per_head((level_count, rows), base),
                pl.BlockSpec((1, lanes), lambda g: (0, g + base)),
            ]
            + [per_head((dim, dim))] * bits
            + [pl.BlockSpec(memory_space=pl.ANY)] * len(done),
            out_specs=wide(base),
            out_shape=jax.ShapeDtypeStruct((rows, width), jnp.bfloat16),
            input_output_aliases={4 + bits: 0} if done else {},
            compiler_params=limit,
            cost_estimate=pl.CostEstimate(
                flops=2 * bits * rows * half_width * dim,
                bytes_accessed=8 * rows * half_width,
                transcendentals=0,
            ),
            name="mix",
        )(queries, within, lam, out_gain.reshape(1, width), *levels, *done)

    first, second = Chain(), Chain()
    keys, values_t = [None] * halves, [None] * halves
    keys[0], values_t[0], first.state = states(0, rim)
    keys[1], values_t[1], second.state = stage(
        [(first, op) for op in first.operations(0)], lambda r: states(1, r), rim
    )
    plan = {}
    for chain, lag in ((first, 0), (second, 1)):
        for bit in range(bits):
            for late, op in enumerate(chain.operations(bit)):
                plan.setdefault(bit + lag + late, []).append((chain, op))
    rounds = max(plan)
    ready = max(turn for turn in plan for chain, _ in plan[turn] if chain is first)
    left = list(range(steps * halves))
    sizes = spread(left, ready)
    done = [[], []]
    for turn in range(1, rounds + 1):
        moves = plan[turn]
        if turn <= ready:
            todo = sizes[turn - 1]

            def run(inputs):
                lam, done = inputs
                done = list(done)
                for start, own in todo:
                    half = start // steps
                    done[half] = inside(
                        start, own, rim, keys[half], values_t[half], lam, done[half]
                    )
                return lam, done

            lam, done = stage(moves, run, (lam, done))
        elif turn == ready + 1:

            def run(inputs):
                lam, (queries, within), levels = inputs
                return mix(0, queries, within, lam, levels, [])

            out = stage(moves, run, (lam, done[0], first.levels()))
        else:
            out = stage(moves, None, out)
    return mix(1, *done[1], lam, second.levels(), [out])


def solution(mesh):
    placed = (P(None, ("groups", "ctx"), None), P(), P(None, None, ("groups", "ctx")), P())
    return jax.shard_map(
        on_device, mesh=mesh, in_specs=placed, out_specs=P(("groups", "ctx"), None), check_vma=False
    )
```

```python
import functools

import jax
import jax.numpy as jnp
from jax import lax
from jax.experimental import pallas as pl
from jax.experimental.pallas import tpu as pltpu
from jax.sharding import PartitionSpec as P

PAD = 8
TILE = 128
NT = (((1,), (1,)), ((), ()))


def convolve(data_ref, rim_ref, taps_ref, held):
    rows = data_ref.shape[1]
    taps = taps_ref.shape[1]
    held[0:PAD, :] = rim_ref[0]
    held[PAD : PAD + rows, :] = data_ref[0].astype(jnp.float32)
    total = taps_ref[0, 0:1, :] * held[PAD - taps + 1 : PAD - taps + 1 + rows, :]
    for tap in range(1, taps):
        first = PAD - taps + 1 + tap
        total = total + taps_ref[0, tap : tap + 1, :] * held[first : first + rows, :]
    return total.astype(jnp.bfloat16)


def state_kernel(dim, k_in, v_in, k_rim, v_rim, k_taps, v_taps, k_out, vt_out, state_out, held):
    k_out[...] = convolve(k_in, k_rim, k_taps, held)
    values = convolve(v_in, v_rim, v_taps, held)
    for head in range(k_out.shape[1] // dim):
        lanes = slice(head * dim, (head + 1) * dim)
        flipped = values[:, lanes].T
        vt_out[lanes, :] = flipped
        state_out[head] = jnp.dot(
            flipped, k_out[:, lanes], preferred_element_type=jnp.float32
        ).astype(jnp.bfloat16)


def tile_weights(lam, rows):
    strip = PAD.bit_length() - 1
    query = lax.rem(lax.broadcasted_iota(jnp.int32, (TILE // PAD, rows), 1), TILE)
    block = lax.broadcasted_iota(jnp.int32, (TILE // PAD, rows), 0)
    differ = lax.bitwise_xor(lax.shift_right_logical(query, strip), block)
    top = TILE.bit_length() - 1
    outer = jnp.broadcast_to(lam[top : top + 1], differ.shape)
    for level in range(top - 1, strip, -1):
        outer = jnp.where(differ < 2 ** (level - strip), lam[level : level + 1], outer)
    outer = jnp.where(block <= lax.shift_right_logical(query, strip), outer, 0.0)
    query8 = lax.rem(lax.broadcasted_iota(jnp.int32, (PAD, rows), 1), PAD)
    key8 = lax.broadcasted_iota(jnp.int32, (PAD, rows), 0)
    differ8 = lax.bitwise_xor(query8, key8)
    inner = jnp.broadcast_to(lam[strip : strip + 1], differ8.shape)
    for level in range(strip - 1, -1, -1):
        inner = jnp.where(differ8 < 2**level, lam[level : level + 1], inner)
    inner = jnp.where(key8 <= query8, inner, 0.0)
    own = lax.shift_right_logical(
        lax.rem(lax.broadcasted_iota(jnp.int32, (PAD, rows), 1), TILE), strip
    )
    return jnp.concatenate(
        [
            jnp.where(own == number, inner, outer[number : number + 1])
            for number in range(TILE // PAD)
        ],
        0,
    )


def inside_kernel(dim, q_in, q_rim, q_taps, k_in, vt_in, lam_in, q_old, in_old, q_out, in_out, held, weights):
    rows = k_in.shape[0]
    tiles = rows // TILE
    q_out[...] = convolve(q_in, q_rim, q_taps, held)
    top = TILE.bit_length() - 1
    pair = min(2, tiles)
    for tile in range(tiles):
        start = tile // pair * pair * TILE
        if start < tile * TILE:
            weights[tile * TILE : (tile + 1) * TILE, start : tile * TILE] = jnp.zeros(
                (TILE, tile * TILE - start), jnp.bfloat16
            )
    for head in range(k_in.shape[1] // dim):
        lanes = slice(head * dim, (head + 1) * dim)
        lam = lam_in[head]
        diagonal = tile_weights(lam, rows)
        for tile in range(tiles):
            keys = slice(tile * TILE, (tile + 1) * TILE)
            scores = lax.dot_general(
                k_in[keys, lanes],
                q_out[tile * TILE :, lanes],
                NT,
                preferred_element_type=jnp.float32,
            )
            for other in range(tile, tiles):
                queries = slice(other * TILE, (other + 1) * TILE)
                part = scores[:, (other - tile) * TILE : (other - tile + 1) * TILE]
                if other == tile:
                    factor = diagonal[:, queries]
                else:
                    level = top + (other ^ tile).bit_length()
                    factor = lam[level : level + 1, queries]
                weights[keys, queries] = (part * factor).astype(jnp.bfloat16)
        for first in range(0, tiles, pair):
            queries = slice(first * TILE, (first + pair) * TILE)
            depth = (first + pair) * TILE
            in_out[lanes, queries] = jnp.dot(
                vt_in[lanes, :depth], weights[:depth, queries], preferred_element_type=jnp.float32
            )


def mix_kernel(dim, base, depths, q_in, in_in, lam_in, gain_in, pieces, out):
    place = pl.program_id(0)
    for head in range(q_in.shape[1] // dim):
        lanes = slice(head * dim, (head + 1) * dim)
        chosen = []
        for shift, refs in zip(depths, pieces):
            value = refs[0][head]
            for index in range(1, len(refs)):
                value = jnp.where((place >> shift) == index, refs[index][head], value)
            chosen.append(value)
        total = in_in[lanes, :]
        products = lax.dot_general(
            jnp.concatenate(chosen, 0), q_in[:, lanes], NT, preferred_element_type=jnp.float32
        )
        for bit in range(len(chosen)):
            product = products[bit * dim : (bit + 1) * dim]
            total = total + lam_in[head, base + bit : base + bit + 1, :] * product
        inverse = lax.rsqrt(jnp.mean(total * total, 0, keepdims=True) + 1e-06)
        normed = (total * inverse).T * gain_in[0:1, lanes]
        out[:, lanes] = normed.astype(jnp.bfloat16)


class Chain:
    def __init__(self, deepest):
        self.count = lax.axis_size("ctx")
        self.bits = self.count.bit_length() - 1
        self.me = lax.axis_index("ctx")
        self.deepest = deepest
        self.state, self.cut, self.got = None, 0, {}

    def depth(self, bit):
        return min((bit + 1) // 2, self.deepest)

    def operations(self, bit):
        return [(bit, offset) for offset in range(2 ** self.depth(bit))]

    def takers(self, bit):
        return [to for to in range(self.count) if bit < self.bits - 1 or to >> bit & 1]

    def outgoing(self, operation):
        bit, offset = operation
        if offset:
            return self.got[bit][0]
        while self.cut < self.depth(bit):
            size = self.state.shape[0] // 2
            start = ((self.me >> self.cut) & 1) * size
            self.state = lax.dynamic_slice_in_dim(self.state, start, size, 0)
            self.cut += 1
        return self.state

    def exchange(self, operation, value):
        bit, offset = operation
        depth = self.depth(bit)
        away = sum(2 ** (depth - 1 - step) for step in range(depth) if offset >> step & 1)
        if not offset:
            away = 2**bit
        return lax.ppermute(value, "ctx", [(to ^ away, to) for to in self.takers(bit)])

    def land(self, operation, value, came):
        bit, offset = operation
        if offset:
            self.got[bit].append(came)
            return
        self.got[bit] = [came]
        if bit < self.bits - 1:
            total = value.astype(jnp.float32) + came.astype(jnp.float32)
            self.state = total.astype(jnp.bfloat16)

    def levels(self):
        return [self.got[bit] for bit in range(self.bits)]


def tie(values):
    return lax.optimization_barrier(values)


def stage(moves, compute, inputs):
    values, inputs = tie(([chain.outgoing(op) for chain, op in moves], inputs))
    came = [chain.exchange(op, value) for (chain, op), value in zip(moves, values)]
    results = compute(inputs) if compute else inputs
    came, values, results = tie((came, values, results))
    for (chain, op), value, new in zip(moves, values, came):
        chain.land(op, value, new)
    return results


def spread(groups, rounds):
    half = len(groups) // 2
    early = rounds // 2
    calls = []
    for base, count in ((0, early), (half, rounds - early)):
        for index in range(count):
            start = -(-half * index // count)
            stop = -(-half * (index + 1) // count)
            calls.append([(base + start, stop - start)] if stop > start else [])
    return calls


def on_device(projected, conv_weight, level_codes, out_gain):
    taps = conv_weight.shape[1]
    rows, width = projected.shape[1:]
    level_count, heads = level_codes.shape[:2]
    dim = width // heads
    tok_bits = rows.bit_length() - 1
    count = lax.axis_size("ctx")
    bits = count.bit_length() - 1
    me = lax.axis_index("ctx")
    group = 4
    lanes = group * dim
    halves = 2
    steps = heads // group // halves
    deepest = steps.bit_length() - 1
    own_bits = sum(((me >> step) & 1) << (deepest - 1 - step) for step in range(deepest))
    order = lax.iota(jnp.int32, steps) ^ own_bits

    rim = lax.ppermute(
        projected[:, rows - taps + 1 :, :], "ctx", [(c, c + 1) for c in range(count - 1)]
    )
    on_bit = (me >> jnp.arange(bits)) & 1
    scale = jnp.concatenate([jnp.ones((tok_bits + 1,), jnp.int32), on_bit])
    lam = (level_codes * scale[:, None, None]).transpose(1, 0, 2).astype(jnp.float32) / 8.0
    rim, lam = tie((rim, lam))
    rim = jnp.pad(rim.astype(jnp.float32), ((0, 0), (PAD - taps + 1, 0), (0, 0)))

    def data(kind, base):
        return [
            pl.BlockSpec((1, rows, lanes), lambda g: (kind, 0, g + base)),
            pl.BlockSpec((1, PAD, lanes), lambda g: (kind, 0, g + base)),
            pl.BlockSpec((1, taps, lanes), lambda g: (kind, 0, g + base)),
        ]

    def wide(base=0):
        return pl.BlockSpec((rows, lanes), lambda g: (0, g + base))

    def tall(base=0):
        return pl.BlockSpec((lanes, rows), lambda g: (g + base, 0))

    def per_head(size, base=0):
        return pl.BlockSpec((group,) + size, lambda g: (g + base, 0, 0))

    held = pltpu.VMEM((PAD + rows, lanes), jnp.float32)
    limit = pltpu.CompilerParams(vmem_limit_bytes=56 * 2**20)
    half_width = width // halves

    def states(half, rim):
        base = half * steps
        return pl.pallas_call(
            functools.partial(state_kernel, dim),
            grid=(steps,),
            in_specs=[s for both in zip(data(1, base), data(2, base)) for s in both],
            out_specs=[wide(), tall(), per_head((dim, dim))],
            out_shape=[
                jax.ShapeDtypeStruct((rows, half_width), jnp.bfloat16),
                jax.ShapeDtypeStruct((half_width, rows), jnp.bfloat16),
                jax.ShapeDtypeStruct((heads // halves, dim, dim), jnp.bfloat16),
            ],
            scratch_shapes=[held],
            compiler_params=limit,
            cost_estimate=pl.CostEstimate(
                flops=2 * rows * half_width * dim,
                bytes_accessed=8 * rows * half_width,
                transcendentals=0,
            ),
            name="states",
        )(projected, projected, rim, rim, conv_weight, conv_weight)

    def inside(first_group, own, rim, keys, values_t, lam, done):
        within = first_group % steps
        share = rows * rows * lanes * own
        call = pl.pallas_call(
            functools.partial(inside_kernel, dim)
            if done
            else lambda *refs: inside_kernel(dim, *refs[:6], None, None, *refs[6:]),
            grid=(own,),
            in_specs=data(0, first_group)
            + [wide(within), tall(within), per_head((level_count, rows), first_group)]
            + [pl.BlockSpec(memory_space=pl.ANY)] * len(done),
            out_specs=[wide(within), tall(within)],
            out_shape=[
                jax.ShapeDtypeStruct((rows, half_width), jnp.bfloat16),
                jax.ShapeDtypeStruct((half_width, rows), jnp.float32),
            ],
            scratch_shapes=[held, pltpu.VMEM((rows, rows), jnp.bfloat16)],
            input_output_aliases={6: 0, 7: 1} if done else {},
            compiler_params=limit,
            cost_estimate=pl.CostEstimate(
                flops=8 * share, bytes_accessed=10 * rows * lanes * own, transcendentals=0
            ),
            name="inside",
        )
        return list(call(projected, rim, conv_weight, keys, values_t, lam, *done))

    def mix(half, queries, within, lam, levels, done):
        base = half * steps
        shifts = [deepest - len(pieces).bit_length() + 1 for pieces in levels]
        flat = [piece for pieces in levels for piece in pieces]

        def kernel(order, q_in, in_in, lam_in, gain_in, *rest):
            rest = list(rest)
            refs = [[rest.pop(0) for _ in pieces] for pieces in levels]
            mix_kernel(
                dim, tok_bits + 1, shifts, q_in, in_in, lam_in, gain_in, refs, rest[-1]
            )

        def piece_spec(shift):
            return pl.BlockSpec(
                (group, dim, dim), lambda g, order: (order[g] & (2**shift - 1), 0, 0)
            )

        return pl.pallas_call(
            kernel,
            grid_spec=pltpu.PrefetchScalarGridSpec(
                num_scalar_prefetch=1,
                grid=(steps,),
                in_specs=[
                    pl.BlockSpec((rows, lanes), lambda g, order: (0, order[g])),
                    pl.BlockSpec((lanes, rows), lambda g, order: (order[g], 0)),
                    pl.BlockSpec(
                        (group, level_count, rows), lambda g, order: (order[g] + base, 0, 0)
                    ),
                    pl.BlockSpec((1, lanes), lambda g, order: (0, order[g] + base)),
                ]
                + [piece_spec(shift) for shift, pieces in zip(shifts, levels) for _ in pieces]
                + [pl.BlockSpec(memory_space=pl.ANY)] * len(done),
                out_specs=pl.BlockSpec((rows, lanes), lambda g, order: (0, order[g] + base)),
            ),
            out_shape=jax.ShapeDtypeStruct((rows, width), jnp.bfloat16),
            input_output_aliases={5 + len(flat): 0} if done else {},
            compiler_params=limit,
            cost_estimate=pl.CostEstimate(
                flops=2 * bits * rows * half_width * dim,
                bytes_accessed=8 * rows * half_width,
                transcendentals=0,
            ),
            name="mix",
        )(order, queries, within, lam, out_gain.reshape(1, width), *flat, *done)

    first, second = Chain(deepest), Chain(deepest)
    keys, values_t = [None] * halves, [None] * halves
    keys[0], values_t[0], first.state = states(0, rim)
    keys[1], values_t[1], second.state = stage(
        [(first, op) for op in first.operations(0)], lambda r: states(1, r), rim
    )
    plan = {}
    for chain, lag in ((first, 0), (second, 1)):
        for bit in range(bits):
            for op in chain.operations(bit):
                plan.setdefault(bit + lag + (op[1] > 0), []).append((chain, op))
    rounds = max(plan)
    ready = max(turn for turn in plan for chain, _ in plan[turn] if chain is first)
    left = list(range(steps * halves))
    sizes = spread(left, ready)
    done = [[], []]
    for turn in range(1, rounds + 1):
        moves = plan[turn]
        if turn <= ready:
            todo = sizes[turn - 1]

            def run(inputs):
                lam, done = inputs
                done = list(done)
                for start, own in todo:
                    half = start // steps
                    done[half] = inside(
                        start, own, rim, keys[half], values_t[half], lam, done[half]
                    )
                return lam, done

            lam, done = stage(moves, run, (lam, done))
        elif turn == ready + 1:

            def run(inputs):
                lam, (queries, within), levels = inputs
                return mix(0, queries, within, lam, levels, [])

            out = stage(moves, run, (lam, done[0], first.levels()))
        else:
            out = stage(moves, None, out)
    return mix(1, *done[1], lam, second.levels(), [out])


def solution(mesh):
    placed = (P(None, ("groups", "ctx"), None), P(), P(None, None, ("groups", "ctx")), P())
    return jax.shard_map(
        on_device, mesh=mesh, in_specs=placed, out_specs=P(("groups", "ctx"), None), check_vma=False
    )
```

```python
import functools

import jax
import jax.numpy as jnp
from jax import lax
from jax.experimental import pallas as pl
from jax.experimental.pallas import tpu as pltpu
from jax.sharding import PartitionSpec as P

PAD = 8
TILE = 128
NT = (((1,), (1,)), ((), ()))


def convolve(data_ref, rim_ref, taps_ref, held):
    rows = data_ref.shape[1]
    taps = taps_ref.shape[1]
    held[PAD - taps + 1 : PAD, :] = rim_ref[0].astype(jnp.float32)
    held[PAD : PAD + rows, :] = data_ref[0].astype(jnp.float32)
    total = taps_ref[0, 0:1, :] * held[PAD - taps + 1 : PAD - taps + 1 + rows, :]
    for tap in range(1, taps):
        first = PAD - taps + 1 + tap
        total = total + taps_ref[0, tap : tap + 1, :] * held[first : first + rows, :]
    return total.astype(jnp.bfloat16)


def state_kernel(dim, k_in, v_in, k_rim, v_rim, k_taps, v_taps, k_out, vt_out, state_out, held):
    k_out[...] = convolve(k_in, k_rim, k_taps, held)
    values = convolve(v_in, v_rim, v_taps, held)
    for head in range(k_out.shape[1] // dim):
        lanes = slice(head * dim, (head + 1) * dim)
        flipped = values[:, lanes].T
        vt_out[lanes, :] = flipped
        state_out[head] = jnp.dot(
            flipped, k_out[:, lanes], preferred_element_type=jnp.float32
        ).astype(jnp.bfloat16)


def tile_weights(lam, rows):
    strip = PAD.bit_length() - 1
    query = lax.rem(lax.broadcasted_iota(jnp.int32, (TILE // PAD, rows), 1), TILE)
    block = lax.broadcasted_iota(jnp.int32, (TILE // PAD, rows), 0)
    differ = lax.bitwise_xor(lax.shift_right_logical(query, strip), block)
    top = TILE.bit_length() - 1
    outer = jnp.broadcast_to(lam[top : top + 1], differ.shape)
    for level in range(top - 1, strip, -1):
        outer = jnp.where(differ < 2 ** (level - strip), lam[level : level + 1], outer)
    outer = jnp.where(block <= lax.shift_right_logical(query, strip), outer, 0.0)
    query8 = lax.rem(lax.broadcasted_iota(jnp.int32, (PAD, rows), 1), PAD)
    key8 = lax.broadcasted_iota(jnp.int32, (PAD, rows), 0)
    differ8 = lax.bitwise_xor(query8, key8)
    inner = jnp.broadcast_to(lam[strip : strip + 1], differ8.shape)
    for level in range(strip - 1, -1, -1):
        inner = jnp.where(differ8 < 2**level, lam[level : level + 1], inner)
    inner = jnp.where(key8 <= query8, inner, 0.0)
    own = lax.shift_right_logical(
        lax.rem(lax.broadcasted_iota(jnp.int32, (PAD, rows), 1), TILE), strip
    )
    return jnp.concatenate(
        [
            jnp.where(own == number, inner, outer[number : number + 1])
            for number in range(TILE // PAD)
        ],
        0,
    )


def inside_kernel(dim, q_in, q_rim, q_taps, k_in, vt_in, lam_in, q_old, in_old, q_out, in_out, held, weights):
    rows = k_in.shape[0]
    tiles = rows // TILE
    q_out[...] = convolve(q_in, q_rim, q_taps, held)
    top = TILE.bit_length() - 1
    pair = min(2, tiles)
    for tile in range(tiles):
        start = tile // pair * pair * TILE
        if start < tile * TILE:
            weights[tile * TILE : (tile + 1) * TILE, start : tile * TILE] = jnp.zeros(
                (TILE, tile * TILE - start), jnp.bfloat16
            )
    for head in range(k_in.shape[1] // dim):
        lanes = slice(head * dim, (head + 1) * dim)
        lam = lam_in[head]
        diagonal = tile_weights(lam, rows)
        for tile in range(tiles):
            keys = slice(tile * TILE, (tile + 1) * TILE)
            scores = lax.dot_general(
                k_in[keys, lanes],
                q_out[tile * TILE :, lanes],
                NT,
                preferred_element_type=jnp.float32,
            )
            for other in range(tile, tiles):
                queries = slice(other * TILE, (other + 1) * TILE)
                part = scores[:, (other - tile) * TILE : (other - tile + 1) * TILE]
                if other == tile:
                    factor = diagonal[:, queries]
                else:
                    level = top + (other ^ tile).bit_length()
                    factor = lam[level : level + 1, queries]
                weights[keys, queries] = (part * factor).astype(jnp.bfloat16)
        for first in range(0, tiles, pair):
            queries = slice(first * TILE, (first + pair) * TILE)
            depth = (first + pair) * TILE
            in_out[lanes, queries] = jnp.dot(
                vt_in[lanes, :depth], weights[:depth, queries], preferred_element_type=jnp.float32
            )


def mix_kernel(dim, base, depths, q_in, in_in, lam_in, gain_in, pieces, out):
    place = pl.program_id(0)
    for head in range(q_in.shape[1] // dim):
        lanes = slice(head * dim, (head + 1) * dim)
        chosen = []
        for shift, refs in zip(depths, pieces):
            value = refs[0][head]
            for index in range(1, len(refs)):
                value = jnp.where((place >> shift) == index, refs[index][head], value)
            chosen.append(value)
        total = in_in[lanes, :]
        products = lax.dot_general(
            jnp.concatenate(chosen, 0), q_in[:, lanes], NT, preferred_element_type=jnp.float32
        )
        for bit in range(len(chosen)):
            product = products[bit * dim : (bit + 1) * dim]
            total = total + lam_in[head, base + bit : base + bit + 1, :] * product
        inverse = lax.rsqrt(jnp.mean(total * total, 0, keepdims=True) + 1e-06)
        normed = (total * inverse).T * gain_in[0:1, lanes]
        out[:, lanes] = normed.astype(jnp.bfloat16)


class Chain:
    def __init__(self, deepest):
        self.count = lax.axis_size("ctx")
        self.bits = self.count.bit_length() - 1
        self.me = lax.axis_index("ctx")
        self.deepest = deepest
        self.state, self.cut, self.got = None, 0, {}

    def depth(self, bit):
        return min((bit + 1) // 2, self.deepest, 1)

    def operations(self, bit):
        return [(bit, offset) for offset in range(2 ** self.depth(bit))]

    def takers(self, bit):
        return [to for to in range(self.count) if bit < self.bits - 1 or to >> bit & 1]

    def outgoing(self, operation):
        bit, offset = operation
        if offset:
            return self.got[bit][0]
        while self.cut < self.depth(bit):
            size = self.state.shape[0] // 2
            start = ((self.me >> self.cut) & 1) * size
            self.state = lax.dynamic_slice_in_dim(self.state, start, size, 0)
            self.cut += 1
        return self.state

    def exchange(self, operation, value):
        bit, offset = operation
        depth = self.depth(bit)
        away = sum(2 ** (depth - 1 - step) for step in range(depth) if offset >> step & 1)
        if not offset:
            away = 2**bit
        return lax.ppermute(value, "ctx", [(to ^ away, to) for to in self.takers(bit)])

    def land(self, operation, value, came):
        bit, offset = operation
        if offset:
            self.got[bit].append(came)
            return
        self.got[bit] = [came]
        if bit < self.bits - 1:
            total = value.astype(jnp.float32) + came.astype(jnp.float32)
            self.state = total.astype(jnp.bfloat16)

    def levels(self):
        return [self.got[bit] for bit in range(self.bits)]


def tie(values):
    return lax.optimization_barrier(values)


def stage(moves, compute, inputs):
    values, inputs = tie(([chain.outgoing(op) for chain, op in moves], inputs))
    came = [chain.exchange(op, value) for (chain, op), value in zip(moves, values)]
    results = compute(inputs) if compute else inputs
    came, values, results = tie((came, values, results))
    for (chain, op), value, new in zip(moves, values, came):
        chain.land(op, value, new)
    return results


def spread(groups, rounds):
    half = len(groups) // 2
    early = rounds // 2
    calls = []
    for base, count in ((0, early), (half, rounds - early)):
        for index in range(count):
            start = -(-half * index // count)
            stop = -(-half * (index + 1) // count)
            calls.append([(base + start, stop - start)] if stop > start else [])
    return calls


def on_device(projected, conv_weight, level_codes, out_gain):
    taps = conv_weight.shape[1]
    rows, width = projected.shape[1:]
    level_count, heads = level_codes.shape[:2]
    dim = width // heads
    tok_bits = rows.bit_length() - 1
    count = lax.axis_size("ctx")
    bits = count.bit_length() - 1
    me = lax.axis_index("ctx")
    group = 4
    lanes = group * dim
    halves = 2
    steps = heads // group // halves
    deepest = steps.bit_length() - 1
    own_bits = sum(((me >> step) & 1) << (deepest - 1 - step) for step in range(deepest))
    order = lax.iota(jnp.int32, steps) ^ own_bits

    rim = lax.ppermute(
        projected[:, rows - taps + 1 :, :], "ctx", [(c, c + 1) for c in range(count - 1)]
    )
    on_bit = (me >> jnp.arange(bits)) & 1
    scale = jnp.concatenate([jnp.ones((tok_bits + 1,), jnp.int32), on_bit])
    lam = (level_codes * scale[:, None, None]).transpose(1, 0, 2).astype(jnp.float32) / 8.0
    rim, lam = tie((rim, lam))

    def data(kind, base):
        return [
            pl.BlockSpec((1, rows, lanes), lambda g: (kind, 0, g + base)),
            pl.BlockSpec((1, taps - 1, lanes), lambda g: (kind, 0, g + base)),
            pl.BlockSpec((1, taps, lanes), lambda g: (kind, 0, g + base)),
        ]

    def wide(base=0):
        return pl.BlockSpec((rows, lanes), lambda g: (0, g + base))

    def tall(base=0):
        return pl.BlockSpec((lanes, rows), lambda g: (g + base, 0))

    def per_head(size, base=0):
        return pl.BlockSpec((group,) + size, lambda g: (g + base, 0, 0))

    held = pltpu.VMEM((PAD + rows, lanes), jnp.float32)
    limit = pltpu.CompilerParams(vmem_limit_bytes=56 * 2**20)
    half_width = width // halves

    def states(half, rim):
        base = half * steps
        return pl.pallas_call(
            functools.partial(state_kernel, dim),
            grid=(steps,),
            in_specs=[s for both in zip(data(1, base), data(2, base)) for s in both],
            out_specs=[wide(), tall(), per_head((dim, dim))],
            out_shape=[
                jax.ShapeDtypeStruct((rows, half_width), jnp.bfloat16),
                jax.ShapeDtypeStruct((half_width, rows), jnp.bfloat16),
                jax.ShapeDtypeStruct((heads // halves, dim, dim), jnp.bfloat16),
            ],
            scratch_shapes=[held],
            compiler_params=limit,
            cost_estimate=pl.CostEstimate(
                flops=2 * rows * half_width * dim,
                bytes_accessed=8 * rows * half_width,
                transcendentals=0,
            ),
            name="states",
        )(projected, projected, rim, rim, conv_weight, conv_weight)

    def inside(first_group, own, rim, keys, values_t, lam, done):
        within = first_group % steps
        share = rows * rows * lanes * own
        call = pl.pallas_call(
            functools.partial(inside_kernel, dim)
            if done
            else lambda *refs: inside_kernel(dim, *refs[:6], None, None, *refs[6:]),
            grid=(own,),
            in_specs=data(0, first_group)
            + [wide(within), tall(within), per_head((level_count, rows), first_group)]
            + [pl.BlockSpec(memory_space=pl.ANY)] * len(done),
            out_specs=[wide(within), tall(within)],
            out_shape=[
                jax.ShapeDtypeStruct((rows, half_width), jnp.bfloat16),
                jax.ShapeDtypeStruct((half_width, rows), jnp.float32),
            ],
            scratch_shapes=[held, pltpu.VMEM((rows, rows), jnp.bfloat16)],
            input_output_aliases={6: 0, 7: 1} if done else {},
            compiler_params=limit,
            cost_estimate=pl.CostEstimate(
                flops=8 * share, bytes_accessed=10 * rows * lanes * own, transcendentals=0
            ),
            name="inside",
        )
        return list(call(projected, rim, conv_weight, keys, values_t, lam, *done))

    def mix(half, queries, within, lam, levels, done):
        base = half * steps
        shifts = [deepest - len(pieces).bit_length() + 1 for pieces in levels]
        flat = [piece for pieces in levels for piece in pieces]

        def kernel(order, q_in, in_in, lam_in, gain_in, *rest):
            rest = list(rest)
            refs = [[rest.pop(0) for _ in pieces] for pieces in levels]
            mix_kernel(
                dim, tok_bits + 1, shifts, q_in, in_in, lam_in, gain_in, refs, rest[-1]
            )

        def piece_spec(shift):
            return pl.BlockSpec(
                (group, dim, dim), lambda g, order: (order[g] & (2**shift - 1), 0, 0)
            )

        return pl.pallas_call(
            kernel,
            grid_spec=pltpu.PrefetchScalarGridSpec(
                num_scalar_prefetch=1,
                grid=(steps,),
                in_specs=[
                    pl.BlockSpec((rows, lanes), lambda g, order: (0, order[g])),
                    pl.BlockSpec((lanes, rows), lambda g, order: (order[g], 0)),
                    pl.BlockSpec(
                        (group, level_count, rows), lambda g, order: (order[g] + base, 0, 0)
                    ),
                    pl.BlockSpec((1, lanes), lambda g, order: (0, order[g] + base)),
                ]
                + [piece_spec(shift) for shift, pieces in zip(shifts, levels) for _ in pieces]
                + [pl.BlockSpec(memory_space=pl.ANY)] * len(done),
                out_specs=pl.BlockSpec((rows, lanes), lambda g, order: (0, order[g] + base)),
            ),
            out_shape=jax.ShapeDtypeStruct((rows, width), jnp.bfloat16),
            input_output_aliases={5 + len(flat): 0} if done else {},
            compiler_params=limit,
            cost_estimate=pl.CostEstimate(
                flops=2 * bits * rows * half_width * dim,
                bytes_accessed=8 * rows * half_width,
                transcendentals=0,
            ),
            name="mix",
        )(order, queries, within, lam, out_gain.reshape(1, width), *flat, *done)

    first, second = Chain(deepest), Chain(deepest)
    keys, values_t = [None] * halves, [None] * halves
    keys[0], values_t[0], first.state = states(0, rim)
    keys[1], values_t[1], second.state = stage(
        [(first, op) for op in first.operations(0)], lambda r: states(1, r), rim
    )
    plan = {}
    for chain, lag in ((first, 0), (second, 1)):
        for bit in range(bits):
            for op in chain.operations(bit):
                plan.setdefault(bit + lag + (op[1] > 0), []).append((chain, op))
    rounds = max(plan)
    ready = max(turn for turn in plan for chain, _ in plan[turn] if chain is first)
    left = list(range(steps * halves))
    sizes = spread(left, ready)
    done = [[], []]
    for turn in range(1, rounds + 1):
        moves = plan[turn]
        if turn <= ready:
            todo = sizes[turn - 1]

            def run(inputs):
                lam, done = inputs
                done = list(done)
                for start, own in todo:
                    half = start // steps
                    done[half] = inside(
                        start, own, rim, keys[half], values_t[half], lam, done[half]
                    )
                return lam, done

            lam, done = stage(moves, run, (lam, done))
        elif turn == ready + 1:

            def run(inputs):
                lam, (queries, within), levels = inputs
                return mix(0, queries, within, lam, levels, [])

            out = stage(moves, run, (lam, done[0], first.levels()))
        else:
            out = stage(moves, None, out)
    return mix(1, *done[1], lam, second.levels(), [out])


def solution(mesh):
    placed = (P(None, ("groups", "ctx"), None), P(), P(None, None, ("groups", "ctx")), P())
    return jax.shard_map(
        on_device, mesh=mesh, in_specs=placed, out_specs=P(("groups", "ctx"), None), check_vma=False
    )
```

```python
import functools

import jax
import jax.numpy as jnp
from jax import lax
from jax.experimental import pallas as pl
from jax.experimental.pallas import tpu as pltpu
from jax.sharding import PartitionSpec as P

PAD = 8
TILE = 128
NT = (((1,), (1,)), ((), ()))


def convolve(data_ref, rim_ref, taps_ref, scratch):
    held, older = scratch.at[0], scratch.at[1]
    rows = data_ref.shape[1]
    taps = taps_ref.shape[1]
    held[PAD - taps + 1 : PAD, :] = rim_ref[0].astype(jnp.float32)
    held[PAD : PAD + rows, :] = data_ref[0].astype(jnp.float32)
    weight = [taps_ref[0, tap : tap + 1, :] for tap in range(taps)]
    last = slice(PAD, PAD + rows)
    before = held[PAD - 1 : PAD - 1 + rows, :]
    if taps == 4:
        older[PAD - 2 : PAD, :] = (
            weight[1] * held[PAD - 2 : PAD, :] + weight[0] * held[PAD - 3 : PAD - 1, :]
        )
        older[last, :] = weight[1] * held[last, :] + weight[0] * before
        total = older[PAD - 2 : PAD - 2 + rows, :]
        total = total + weight[2] * before + weight[3] * held[last, :]
    else:
        total = weight[0] * held[PAD - taps + 1 : PAD - taps + 1 + rows, :]
        for tap in range(1, taps):
            first = PAD - taps + 1 + tap
            total = total + weight[tap] * held[first : first + rows, :]
    return total.astype(jnp.bfloat16)


def state_kernel(dim, k_in, v_in, k_rim, v_rim, k_taps, v_taps, k_out, vt_out, state_out, held):
    k_out[...] = convolve(k_in, k_rim, k_taps, held)
    values = convolve(v_in, v_rim, v_taps, held)
    for head in range(k_out.shape[1] // dim):
        lanes = slice(head * dim, (head + 1) * dim)
        flipped = values[:, lanes].T
        vt_out[lanes, :] = flipped
        state_out[head] = jnp.dot(
            flipped, k_out[:, lanes], preferred_element_type=jnp.float32
        ).astype(jnp.bfloat16)


def tile_weights(lam, rows):
    strip = PAD.bit_length() - 1
    query = lax.rem(lax.broadcasted_iota(jnp.int32, (TILE // PAD, rows), 1), TILE)
    block = lax.broadcasted_iota(jnp.int32, (TILE // PAD, rows), 0)
    differ = lax.bitwise_xor(lax.shift_right_logical(query, strip), block)
    top = TILE.bit_length() - 1
    outer = jnp.broadcast_to(lam[top : top + 1], differ.shape)
    for level in range(top - 1, strip, -1):
        outer = jnp.where(differ < 2 ** (level - strip), lam[level : level + 1], outer)
    outer = jnp.where(block <= lax.shift_right_logical(query, strip), outer, 0.0)
    query8 = lax.rem(lax.broadcasted_iota(jnp.int32, (PAD, rows), 1), PAD)
    key8 = lax.broadcasted_iota(jnp.int32, (PAD, rows), 0)
    differ8 = lax.bitwise_xor(query8, key8)
    inner = jnp.broadcast_to(lam[strip : strip + 1], differ8.shape)
    for level in range(strip - 1, -1, -1):
        inner = jnp.where(differ8 < 2**level, lam[level : level + 1], inner)
    inner = jnp.where(key8 <= query8, inner, 0.0)
    own = lax.shift_right_logical(
        lax.rem(lax.broadcasted_iota(jnp.int32, (PAD, rows), 1), TILE), strip
    )
    return jnp.concatenate(
        [
            jnp.where(own == number, inner, outer[number : number + 1])
            for number in range(TILE // PAD)
        ],
        0,
    )


def inside_kernel(dim, q_in, q_rim, q_taps, k_in, vt_in, lam_in, q_old, in_old, q_out, in_out, held, weights):
    rows = k_in.shape[0]
    tiles = rows // TILE
    q_out[...] = convolve(q_in, q_rim, q_taps, held)
    top = TILE.bit_length() - 1
    pair = min(2, tiles)
    for tile in range(tiles):
        start = tile // pair * pair * TILE
        if start < tile * TILE:
            weights[tile * TILE : (tile + 1) * TILE, start : tile * TILE] = jnp.zeros(
                (TILE, tile * TILE - start), jnp.bfloat16
            )
    for head in range(k_in.shape[1] // dim):
        lanes = slice(head * dim, (head + 1) * dim)
        lam = lam_in[head]
        diagonal = tile_weights(lam, rows)
        for tile in range(tiles):
            keys = slice(tile * TILE, (tile + 1) * TILE)
            scores = lax.dot_general(
                k_in[keys, lanes],
                q_out[tile * TILE :, lanes],
                NT,
                preferred_element_type=jnp.float32,
            )
            for other in range(tile, tiles):
                queries = slice(other * TILE, (other + 1) * TILE)
                part = scores[:, (other - tile) * TILE : (other - tile + 1) * TILE]
                if other == tile:
                    factor = diagonal[:, queries]
                else:
                    level = top + (other ^ tile).bit_length()
                    factor = lam[level : level + 1, queries]
                weights[keys, queries] = (part * factor).astype(jnp.bfloat16)
        for first in range(0, tiles, pair):
            queries = slice(first * TILE, (first + pair) * TILE)
            depth = (first + pair) * TILE
            in_out[lanes, queries] = jnp.dot(
                vt_in[lanes, :depth], weights[:depth, queries], preferred_element_type=jnp.float32
            )


def mix_kernel(dim, base, depths, q_in, in_in, lam_in, gain_in, pieces, out):
    place = pl.program_id(0)
    for head in range(q_in.shape[1] // dim):
        lanes = slice(head * dim, (head + 1) * dim)
        chosen = []
        for shift, refs in zip(depths, pieces):
            value = refs[0][head]
            for index in range(1, len(refs)):
                value = jnp.where((place >> shift) == index, refs[index][head], value)
            chosen.append(value)
        total = in_in[lanes, :]
        products = lax.dot_general(
            jnp.concatenate(chosen, 0), q_in[:, lanes], NT, preferred_element_type=jnp.float32
        )
        for bit in range(len(chosen)):
            product = products[bit * dim : (bit + 1) * dim]
            total = total + lam_in[head, base + bit : base + bit + 1, :] * product
        inverse = lax.rsqrt(jnp.mean(total * total, 0, keepdims=True) + 1e-06)
        normed = (total * inverse).T * gain_in[0:1, lanes]
        out[:, lanes] = normed.astype(jnp.bfloat16)


class Chain:
    def __init__(self, deepest):
        self.count = lax.axis_size("ctx")
        self.bits = self.count.bit_length() - 1
        self.me = lax.axis_index("ctx")
        self.deepest = deepest
        self.state, self.cut, self.got = None, 0, {}

    def depth(self, bit):
        return min((bit + 1) // 2, self.deepest, 1)

    def operations(self, bit):
        return [(bit, offset) for offset in range(2 ** self.depth(bit))]

    def takers(self, bit):
        return [to for to in range(self.count) if bit < self.bits - 1 or to >> bit & 1]

    def outgoing(self, operation):
        bit, offset = operation
        if offset:
            return self.got[bit][0]
        while self.cut < self.depth(bit):
            size = self.state.shape[0] // 2
            start = ((self.me >> self.cut) & 1) * size
            self.state = lax.dynamic_slice_in_dim(self.state, start, size, 0)
            self.cut += 1
        return self.state

    def exchange(self, operation, value):
        bit, offset = operation
        depth = self.depth(bit)
        away = sum(2 ** (depth - 1 - step) for step in range(depth) if offset >> step & 1)
        if not offset:
            away = 2**bit
        return lax.ppermute(value, "ctx", [(to ^ away, to) for to in self.takers(bit)])

    def land(self, operation, value, came):
        bit, offset = operation
        if offset:
            self.got[bit].append(came)
            return
        self.got[bit] = [came]
        if bit < self.bits - 1:
            total = value.astype(jnp.float32) + came.astype(jnp.float32)
            self.state = total.astype(jnp.bfloat16)

    def levels(self):
        return [self.got[bit] for bit in range(self.bits)]


def tie(values):
    return lax.optimization_barrier(values)


def stage(moves, compute, inputs):
    values, inputs = tie(([chain.outgoing(op) for chain, op in moves], inputs))
    came = [chain.exchange(op, value) for (chain, op), value in zip(moves, values)]
    results = compute(inputs) if compute else inputs
    came, values, results = tie((came, values, results))
    for (chain, op), value, new in zip(moves, values, came):
        chain.land(op, value, new)
    return results


def spread(groups, rounds):
    half = len(groups) // 2
    early = rounds // 2
    calls = []
    for base, count in ((0, early), (half, rounds - early)):
        for index in range(count):
            start = -(-half * index // count)
            stop = -(-half * (index + 1) // count)
            calls.append([(base + start, stop - start)] if stop > start else [])
    return calls


def on_device(projected, conv_weight, level_codes, out_gain):
    taps = conv_weight.shape[1]
    rows, width = projected.shape[1:]
    level_count, heads = level_codes.shape[:2]
    dim = width // heads
    tok_bits = rows.bit_length() - 1
    count = lax.axis_size("ctx")
    bits = count.bit_length() - 1
    me = lax.axis_index("ctx")
    group = 4
    lanes = group * dim
    halves = 2
    steps = heads // group // halves
    deepest = steps.bit_length() - 1
    own_bits = sum(((me >> step) & 1) << (deepest - 1 - step) for step in range(deepest))
    order = lax.iota(jnp.int32, steps) ^ own_bits

    rim = lax.ppermute(
        projected[:, rows - taps + 1 :, :], "ctx", [(c, c + 1) for c in range(count - 1)]
    )
    on_bit = (me >> jnp.arange(bits)) & 1
    scale = jnp.concatenate([jnp.ones((tok_bits + 1,), jnp.int32), on_bit])
    lam = (level_codes * scale[:, None, None]).transpose(1, 0, 2).astype(jnp.float32) / 8.0
    rim, lam = tie((rim, lam))

    def data(kind, base):
        return [
            pl.BlockSpec((1, rows, lanes), lambda g: (kind, 0, g + base)),
            pl.BlockSpec((1, taps - 1, lanes), lambda g: (kind, 0, g + base)),
            pl.BlockSpec((1, taps, lanes), lambda g: (kind, 0, g + base)),
        ]

    def wide(base=0):
        return pl.BlockSpec((rows, lanes), lambda g: (0, g + base))

    def tall(base=0):
        return pl.BlockSpec((lanes, rows), lambda g: (g + base, 0))

    def per_head(size, base=0):
        return pl.BlockSpec((group,) + size, lambda g: (g + base, 0, 0))

    held = pltpu.VMEM((2, PAD + rows, lanes), jnp.float32)
    limit = pltpu.CompilerParams(vmem_limit_bytes=56 * 2**20)
    half_width = width // halves

    def states(half, rim):
        base = half * steps
        return pl.pallas_call(
            functools.partial(state_kernel, dim),
            grid=(steps,),
            in_specs=[s for both in zip(data(1, base), data(2, base)) for s in both],
            out_specs=[wide(), tall(), per_head((dim, dim))],
            out_shape=[
                jax.ShapeDtypeStruct((rows, half_width), jnp.bfloat16),
                jax.ShapeDtypeStruct((half_width, rows), jnp.bfloat16),
                jax.ShapeDtypeStruct((heads // halves, dim, dim), jnp.bfloat16),
            ],
            scratch_shapes=[held],
            compiler_params=limit,
            cost_estimate=pl.CostEstimate(
                flops=2 * rows * half_width * dim,
                bytes_accessed=8 * rows * half_width,
                transcendentals=0,
            ),
            name="states",
        )(projected, projected, rim, rim, conv_weight, conv_weight)

    def inside(first_group, own, rim, keys, values_t, lam, done):
        within = first_group % steps
        share = rows * rows * lanes * own
        call = pl.pallas_call(
            functools.partial(inside_kernel, dim)
            if done
            else lambda *refs: inside_kernel(dim, *refs[:6], None, None, *refs[6:]),
            grid=(own,),
            in_specs=data(0, first_group)
            + [wide(within), tall(within), per_head((level_count, rows), first_group)]
            + [pl.BlockSpec(memory_space=pl.ANY)] * len(done),
            out_specs=[wide(within), tall(within)],
            out_shape=[
                jax.ShapeDtypeStruct((rows, half_width), jnp.bfloat16),
                jax.ShapeDtypeStruct((half_width, rows), jnp.float32),
            ],
            scratch_shapes=[held, pltpu.VMEM((rows, rows), jnp.bfloat16)],
            input_output_aliases={6: 0, 7: 1} if done else {},
            compiler_params=limit,
            cost_estimate=pl.CostEstimate(
                flops=8 * share, bytes_accessed=10 * rows * lanes * own, transcendentals=0
            ),
            name="inside",
        )
        return list(call(projected, rim, conv_weight, keys, values_t, lam, *done))

    def mix(half, queries, within, lam, levels, done):
        base = half * steps
        shifts = [deepest - len(pieces).bit_length() + 1 for pieces in levels]
        flat = [piece for pieces in levels for piece in pieces]

        def kernel(order, q_in, in_in, lam_in, gain_in, *rest):
            rest = list(rest)
            refs = [[rest.pop(0) for _ in pieces] for pieces in levels]
            mix_kernel(
                dim, tok_bits + 1, shifts, q_in, in_in, lam_in, gain_in, refs, rest[-1]
            )

        def piece_spec(shift):
            return pl.BlockSpec(
                (group, dim, dim), lambda g, order: (order[g] & (2**shift - 1), 0, 0)
            )

        return pl.pallas_call(
            kernel,
            grid_spec=pltpu.PrefetchScalarGridSpec(
                num_scalar_prefetch=1,
                grid=(steps,),
                in_specs=[
                    pl.BlockSpec((rows, lanes), lambda g, order: (0, order[g])),
                    pl.BlockSpec((lanes, rows), lambda g, order: (order[g], 0)),
                    pl.BlockSpec(
                        (group, level_count, rows), lambda g, order: (order[g] + base, 0, 0)
                    ),
                    pl.BlockSpec((1, lanes), lambda g, order: (0, order[g] + base)),
                ]
                + [piece_spec(shift) for shift, pieces in zip(shifts, levels) for _ in pieces]
                + [pl.BlockSpec(memory_space=pl.ANY)] * len(done),
                out_specs=pl.BlockSpec((rows, lanes), lambda g, order: (0, order[g] + base)),
            ),
            out_shape=jax.ShapeDtypeStruct((rows, width), jnp.bfloat16),
            input_output_aliases={5 + len(flat): 0} if done else {},
            compiler_params=limit,
            cost_estimate=pl.CostEstimate(
                flops=2 * bits * rows * half_width * dim,
                bytes_accessed=8 * rows * half_width,
                transcendentals=0,
            ),
            name="mix",
        )(order, queries, within, lam, out_gain.reshape(1, width), *flat, *done)

    first, second = Chain(deepest), Chain(deepest)
    keys, values_t = [None] * halves, [None] * halves
    keys[0], values_t[0], first.state = states(0, rim)
    keys[1], values_t[1], second.state = stage(
        [(first, op) for op in first.operations(0)], lambda r: states(1, r), rim
    )
    plan = {}
    for chain, lag in ((first, 0), (second, 1)):
        for bit in range(bits):
            for op in chain.operations(bit):
                plan.setdefault(bit + lag + (op[1] > 0), []).append((chain, op))
    rounds = max(plan)
    ready = max(turn for turn in plan for chain, _ in plan[turn] if chain is first)
    left = list(range(steps * halves))
    sizes = spread(left, ready)
    done = [[], []]
    for turn in range(1, rounds + 1):
        moves = plan[turn]
        if turn <= ready:
            todo = sizes[turn - 1]

            def run(inputs):
                lam, done = inputs
                done = list(done)
                for start, own in todo:
                    half = start // steps
                    done[half] = inside(
                        start, own, rim, keys[half], values_t[half], lam, done[half]
                    )
                return lam, done

            lam, done = stage(moves, run, (lam, done))
        elif turn == ready + 1:

            def run(inputs):
                lam, (queries, within), levels = inputs
                return mix(0, queries, within, lam, levels, [])

            out = stage(moves, run, (lam, done[0], first.levels()))
        else:
            out = stage(moves, None, out)
    return mix(1, *done[1], lam, second.levels(), [out])


def solution(mesh):
    placed = (P(None, ("groups", "ctx"), None), P(), P(None, None, ("groups", "ctx")), P())
    return jax.shard_map(
        on_device, mesh=mesh, in_specs=placed, out_specs=P(("groups", "ctx"), None), check_vma=False
    )
```
